128 devices in a mesh: fsdp: 4 (over y_lo, core), expert: 32 (over z, y_hi, x).
Axes of the slice: x: 4, y: 4 (y_hi: 2, y_lo: 2; y = y_hi * 2 + y_lo), z: 4, core: 2. Of those that a mesh axis runs over, the one named last changes fastest.
Arguments:
- tokens: bfloat16 [3, 512, 7168], P(None, 'expert'), may hold values from -6 to 6
- route_ids: int32 [3, 512, 8], P(None, 'expert'), may hold values from 0 to 31, all different within a row; in each aligned block of 16 rows (0 to 15, 16 to 31, ..., all dimensions but the last counted through in order) at most 6 rows name the same one
- gate_values: bfloat16 [3, 512, 8], P(None, 'expert'), may hold values from 0.25 to 1
- cap_limit: int32 [32], replicated, may hold values from 3 to 6
- update_ids: int32 [32], replicated, may hold values from 0 to 31, each once
- expert_weights: bfloat16 [32, 7168, 3072], P(None, ('fsdp', 'expert')), may hold values from -0.109375 to 0.109375
Outputs:
- moe_output: bfloat16 [3, 512, 7168], P(None, 'expert', 'fsdp')
The draws below stay inside these ranges and needn't reach their ends.
Inputs may be any that keep to these rules, and one draw needn't show every extreme that they name: `route_ids`: each row names 8 different experts. In every aligned block of 16 rows of one step (the rows of one device) no expert is named by more than 6 rows, a bound that some block reaches. `update_ids`: each expert once.
All inputs are finite; a program needn't handle non-finite values.
Results may differ from the reference program's by a relative error of at most 0.0058.
Values may be sent and summed in bfloat16 or wider, within the bound.
No kernel may reach another device: no remote copies, remote signals or barrier semaphores. Data moves between devices by JAX's collectives and lax.ppermute only.
A program may use at most 128 MiB of HBM per device.

```python
import math
import jax
import jax.numpy as jnp
import numpy as np
from jax import lax

D = 7168
H = 1024
TOP = 8
STEPS = 3
ROWS_DEV = 16
EXPERTS = 32
ROWS = 512
CAP = 6
N_EXPERT = 32


def draw_cap_limit(key, part):
    first_key = jax.random.fold_in(key, 11)
    second_key = jax.random.fold_in(key, 23)
    reduction = jax.random.randint(first_key, (EXPERTS,), 0, CAP // 2 + 1)
    chosen = jax.random.randint(second_key, (), 0, EXPERTS)
    index_row = jnp.arange(EXPERTS, dtype=jnp.int32)
    reduction = jnp.where(index_row == chosen, 0, reduction)
    reduction = jnp.where(index_row == (chosen + 1) % EXPERTS, CAP // 2, reduction)
    return (CAP - reduction).astype(jnp.int32)


def level_of(rng, shape, split, least, top_value):
    def one(axis_at, parts):
        draws = jax.random.uniform(jax.random.fold_in(jax.random.fold_in(rng, 6), axis_at), (parts,), jnp.float32, least / len(split), top_value / len(split))
        return jnp.repeat(jnp.exp(draws), shape[axis_at] // parts).reshape((-1,) + (1,) * (len(shape) - axis_at - 1))

    gain = one(*split[0])
    for cut in split[1:]:
        gain = gain * one(*cut)
    return gain


def assign_block(own_key, own, number, rows, amount, top, limit, lean):
    order = jax.random.permutation(own_key, amount)
    packed, common = portions_of(amount, rows * top, limit, lean, True), portions_of(amount, rows * top, limit, lean, False)
    places = jnp.arange(amount)

    def named(sizes, turn):
        used = int((sizes > 0).sum())
        fixed = max(1, used // 4)
        shifted = fixed + (places - fixed + turn * (used - fixed)) % max(1, amount - fixed)
        return jnp.zeros((amount,), jnp.int32).at[order[jnp.where(places < fixed, places, shifted)]].set(jnp.asarray(sizes, jnp.int32))

    sizes = jnp.where(number % 4 == 0, named(packed, number // 4), named(common, number - number // 4 - 1))
    mixed = jax.random.permutation(jax.random.fold_in(own, 3), amount)
    source_of, receiver = mixed[0:amount // 2 * 2:2], mixed[1:amount // 2 * 2:2]
    slack = jnp.minimum(sizes[source_of] - 1, limit - sizes[receiver]) // 2
    slack = jnp.where((source_of == order[0]) | (receiver == order[0]) | (sizes[receiver] == 0), 0, jnp.maximum(slack, 0))
    shifted = jax.random.randint(jax.random.fold_in(own, 4), (amount // 2,), 0, 1 << 20) % (slack + 1)
    sizes = sizes.at[source_of].add(-shifted).at[receiver].add(shifted)
    labels = jnp.searchsorted(jnp.cumsum(sizes), jnp.arange(rows * top), side="right").astype(jnp.int32)
    grid = labels.reshape(top, rows).T
    grid = grid[jax.random.permutation(jax.random.fold_in(own, 1), rows)]
    turn = jax.random.randint(jax.random.fold_in(own, 2), (rows, 1), 0, top)
    return jnp.take_along_axis(grid, (jnp.arange(top)[None, :] + turn) % top, axis=1)


def portions_of(amount, total, most, skew, full):
    loads = [(1 << 20) // math.isqrt(standing ** skew) + 1 for standing in range(1, amount + 1)]
    largest = most if full else min(most, max(-(-total // amount), total * loads[0] // sum(loads)))
    least = 1 if total - largest >= amount - 1 else 0
    holding, spare = [largest] + [least] * (amount - 1), total - largest - least * (amount - 1)
    while spare > 0:
        candidates = [i for i in range(1, amount) if holding[i] < largest] or [i for i in range(1, amount) if holding[i] < most]
        pool, budget = sum([loads[i] for i in candidates]), spare
        for i in candidates:
            addition = min(most - holding[i], max(1, budget * loads[i] // pool), spare)
            holding[i] = holding[i] + addition
            spare = spare - addition
    return np.array(holding)


def noise(key, shape, scale, bound, pieces=(), kind=jnp.bfloat16):
    values = jax.random.normal(key, shape, jnp.float32) * scale
    if len(pieces) > 0:
        values = level_of(key, shape, pieces, -0.22, 0.18) * values
    return jnp.clip(values, min=-bound, max=bound).astype(kind)


def setup_inputs(seed: int = 0) -> dict:
    key_of = jax.random.split(jax.random.key(seed), 7)
    tokens = noise(key_of[0], (STEPS, ROWS, D), 1.0, 6.0, ((1, 32),))
    route_ids_keys = jax.random.split(jax.random.fold_in(key_of[1], 1), STEPS * ROWS // ROWS_DEV)
    route_ids_turns = jax.random.permutation(jax.random.fold_in(key_of[1], 3), STEPS * ROWS // ROWS_DEV)
    route_ids = jax.vmap(lambda own, number: assign_block(jax.random.fold_in(key_of[1], 2), own, number, ROWS_DEV, EXPERTS, TOP, CAP, 2))(route_ids_keys, route_ids_turns).reshape((STEPS, ROWS, TOP))
    gate_values = jnp.clip(0.25 + 0.75 * jax.random.uniform(key_of[2], (STEPS, ROWS, TOP), jnp.float32) ** level_of(key_of[2], (STEPS, ROWS, TOP), ((1, 32),), -0.2, 0.2), 0.25, 1.0).astype(jnp.bfloat16)
    cap_limit = draw_cap_limit(jax.random.fold_in(key_of[6], 71), 0)
    update_ids = jax.random.permutation(key_of[4], EXPERTS).astype(jnp.int32)
    expert_weights = noise(key_of[5], (EXPERTS, D, 3 * H), (3 * H) ** -0.5, 0.109375, ((1, 128),))
    return {"tokens": tokens, "route_ids": route_ids, "gate_values": gate_values, "cap_limit": cap_limit, "update_ids": update_ids, "expert_weights": expert_weights}


def ffn_rows(rows_in, weights, hidden_all):
    gate_part = jnp.dot(rows_in, weights[:, :hidden_all], preferred_element_type=jnp.float32)
    up_part = jnp.dot(rows_in, weights[:, hidden_all:2 * hidden_all], preferred_element_type=jnp.float32)
    hidden = (jax.nn.silu(gate_part) * up_part).astype(jnp.bfloat16)
    return lax.dot_general(hidden, weights[:, 2 * hidden_all:], (((1,), (1,)), ((), ())), preferred_element_type=jnp.float32).astype(jnp.bfloat16)


def reference(tokens, route_ids, gate_values, cap_limit, update_ids, expert_weights):
    inverse_order = jnp.argsort(update_ids).astype(jnp.int32)
    ordered = jnp.take(expert_weights, inverse_order, axis=0)
    blocks = N_EXPERT
    per_block = ROWS_DEV * TOP
    total_slots = blocks * CAP
    outputs = []
    for step_index in range(STEPS):
        ids_block = route_ids[step_index].reshape(blocks, per_block).astype(jnp.int32)
        expert_hot = (ids_block[:, :, None] == jnp.arange(EXPERTS, dtype=jnp.int32)[None, None, :]).astype(jnp.int32)
        position = jnp.sum((jnp.cumsum(expert_hot, axis=1) - 1) * expert_hot, axis=2).astype(jnp.int32)
        limit_row = jnp.take(cap_limit, ids_block, axis=0)
        kept_mask = position < limit_row
        block_index = jnp.arange(blocks, dtype=jnp.int32)[:, None]
        global_slot = ids_block * total_slots + block_index * CAP + position
        row_global = block_index * ROWS_DEV + jnp.arange(per_block, dtype=jnp.int32)[None, :] // TOP
        target = jnp.where(kept_mask, global_slot, EXPERTS * total_slots).astype(jnp.int32)
        source_row = jnp.full((EXPERTS * total_slots,), ROWS, jnp.int32).at[target.reshape(-1)].set(row_global.reshape(-1).astype(jnp.int32), mode="drop")
        padded_tokens = jnp.concatenate([tokens[step_index], jnp.zeros((1, D), jnp.bfloat16)], axis=0)
        gathered = jnp.take(padded_tokens, source_row, axis=0).reshape(EXPERTS, total_slots, D)
        expert_out = lax.map(lambda operands: ffn_rows(operands[0], operands[1], H), (gathered, ordered))
        flat_out = jnp.concatenate([expert_out.reshape(EXPERTS * total_slots, D), jnp.zeros((1, D), jnp.bfloat16)], axis=0)
        picked = jnp.take(flat_out, target.reshape(-1), axis=0).astype(jnp.float32)
        weight_flat = gate_values[step_index].reshape(-1).astype(jnp.float32)
        mixed_rows = jnp.sum((picked * weight_flat[:, None]).reshape(ROWS, TOP, D), axis=1)
        outputs.append(mixed_rows.astype(jnp.bfloat16))
    return jnp.stack(outputs)
```

```python
import jax
import jax.numpy as jnp
from jax import lax
from jax.experimental import pallas as pl
from jax.experimental.pallas import tpu as pltpu
from jax.sharding import PartitionSpec as P


CORE_SWAP = ((0, 1), (1, 0), (2, 3), (3, 2))
CHIP_SWAP = ((0, 2), (2, 0), (1, 3), (3, 1))


def routing(route_ids, gate_values, cap_limit, update_ids, slot_count):
    steps, rows, top = route_ids.shape
    experts = cap_limit.shape[0]
    choices = steps * rows * top
    flat_ids = route_ids.reshape(choices)
    hot = (flat_ids[:, None] == jnp.arange(experts, dtype=jnp.int32)[None, :]).astype(jnp.bfloat16)
    number = jnp.arange(choices, dtype=jnp.int32)
    per_step = rows * top
    earlier = (number[:, None] > number[None, :]) & (
        number[:, None] // per_step == number[None, :] // per_step
    )
    before = jnp.dot(earlier.astype(jnp.bfloat16), hot, preferred_element_type=jnp.float32)
    hot32 = hot.astype(jnp.float32)
    position = jnp.sum(before * hot32, axis=1).astype(jnp.int32)
    limit = jnp.sum(hot32 * cap_limit.astype(jnp.float32)[None, :], axis=1).astype(jnp.int32)
    holder = jnp.sum(
        jnp.where(
            update_ids[:, None] == jnp.arange(experts, dtype=jnp.int32)[None, :],
            jnp.arange(experts, dtype=jnp.int32)[:, None],
            0,
        ),
        axis=0,
    )
    owner = jnp.sum(hot32 * holder.astype(jnp.float32)[None, :], axis=1).astype(jnp.int32)
    count = steps * slot_count
    first = 16
    within = (number // per_step) * slot_count + position
    slot = jnp.where(
        within < first,
        owner * first + within,
        experts * first + owner * (count - first) + within - first,
    )
    slot = jnp.where(position < limit, slot, -1).reshape(steps * rows, top)
    total = experts * count
    at = jnp.arange(total, dtype=jnp.int32)
    gates = gate_values.reshape(steps * rows, top).astype(jnp.float32)
    dispatch = jnp.zeros((total, steps * rows), jnp.float32)
    combine = jnp.zeros((steps * rows, total), jnp.float32)
    for k in range(top):
        dispatch = dispatch + (at[:, None] == slot[:, k][None, :]).astype(jnp.float32)
        combine = combine + jnp.where(at[None, :] == slot[:, k][:, None], gates[:, k][:, None], 0.0)
    return dispatch.astype(jnp.bfloat16), combine.astype(jnp.bfloat16)


def exchange(block):
    return lax.all_to_all(block, "expert", split_axis=0, concat_axis=0, tiled=True)


def pack_kernel(weights_ref, beside_ref, first_ref, second_ref):
    wide = weights_ref.shape[2] // 3 * 2
    first_ref[:, :, :wide] = weights_ref[:, :, :wide]
    first_ref[:, :, wide:] = beside_ref[...]
    second_ref[...] = weights_ref[:, :, wide:]


def pack(weights, beside):
    experts, local, columns = weights.shape
    hidden = columns // 3
    extra = beside.shape[2]
    batch = 4
    block = lambda width: pl.BlockSpec((batch, local, width), lambda i: (i, 0, 0))
    return pl.pallas_call(
        pack_kernel,
        grid=(experts // batch,),
        in_specs=[block(columns), block(extra)],
        out_specs=[block(2 * hidden + extra), block(hidden)],
        out_shape=[
            jax.ShapeDtypeStruct((experts, local, 2 * hidden + extra), weights.dtype),
            jax.ShapeDtypeStruct((experts, local, hidden), weights.dtype),
        ],
        name="pack",
    )(weights, beside)


def gate_up_kernel(core_ref, arrived_ref, passed_ref, kept_ref, weights, rows, tail, sems):
    experts, local, _ = arrived_ref.shape
    quarter = weights.shape[3]
    wide = 4 * quarter
    share = rows.shape[2]
    main = experts * 16
    core = core_ref[0]
    copies = [
        pltpu.make_async_copy(
            arrived_ref.at[:, pl.ds(16 * b, 16), pl.ds(wide, w)],
            rows.at[:, :, pl.ds(640 * b, w)],
            sems.at[b],
        )
        for b, w in enumerate((640, 640, share - 1280))
    ]
    copies.append(
        pltpu.make_async_copy(arrived_ref.at[:, pl.ds(48, 8), pl.ds(wide, 512)], tail, sems.at[3])
    )
    starts = [(1 - core) * quarter, (1 - core) * quarter + 2 * quarter]
    starts += [core * quarter, core * quarter + 2 * quarter]
    for i, start in enumerate(starts):
        copies.append(
            pltpu.make_async_copy(
                arrived_ref.at[:, :, pl.ds(pl.multiple_of(start, quarter), quarter)],
                weights.at[i],
                sems.at[4 + i],
            )
        )
    for copy in copies:
        copy.start()
    for copy in copies[:4]:
        copy.wait()
    top = rows[...].reshape(main, share)
    flat = tail[...].reshape(experts * 8, 512)
    at = lax.broadcasted_iota(jnp.int32, (2 * experts, 8 * experts), 0)
    of = lax.broadcasted_iota(jnp.int32, (2 * experts, 8 * experts), 1)
    pieces = []
    for q in range(4):
        pick = (of == at * 4 + q).astype(jnp.bfloat16)
        pieces.append(jnp.dot(pick, flat, preferred_element_type=jnp.float32).astype(jnp.bfloat16))
    last = jnp.concatenate(pieces, axis=1)[:, :share]
    for i in range(4):
        copies[4 + i].wait()
        block = weights[i].reshape(experts * local, quarter)
        out_ref = passed_ref if i < 2 else kept_ref
        columns = pl.ds((i % 2) * quarter, quarter)
        out_ref[:main, columns] = jnp.dot(top, block, preferred_element_type=jnp.float32)
        out_ref[main:, columns] = jnp.dot(last, block, preferred_element_type=jnp.float32)


def gate_up(core, arrived, hidden, share):
    experts, local, _ = arrived.shape
    slots = experts * 18
    quarter = hidden // 2
    out = jax.ShapeDtypeStruct((slots, hidden), jnp.float32)
    return pl.pallas_call(
        gate_up_kernel,
        in_specs=[
            pl.BlockSpec(memory_space=pltpu.SMEM),
            pl.BlockSpec(memory_space=pl.ANY),
        ],
        out_specs=[pl.BlockSpec(memory_space=pltpu.VMEM)] * 2,
        out_shape=[out, out],
        scratch_shapes=[
            pltpu.VMEM((4, experts, local, quarter), jnp.bfloat16),
            pltpu.VMEM((experts, 16, share), jnp.bfloat16),
            pltpu.VMEM((experts, 8, 512), jnp.bfloat16),
            pltpu.SemaphoreType.DMA((8,)),
        ],
        compiler_params=pltpu.CompilerParams(vmem_limit_bytes=40 << 20),
        cost_estimate=pl.CostEstimate(
            flops=2 * slots * share * 2 * hidden,
            bytes_accessed=2 * arrived.size + 8 * slots * hidden,
            transcendentals=0,
        ),
        name="gate_up",
    )(core, arrived)


def layer(tokens, route_ids, gate_values, cap_limit, update_ids, expert_weights):
    steps, rows, width = tokens.shape
    experts, _, _ = expert_weights.shape
    fsdp_count = lax.axis_size("fsdp")
    fsdp_at = lax.axis_index("fsdp")
    slot_count = 6
    hidden = expert_weights.shape[2] // 3
    half = hidden // 2
    quarter = half // 2
    share = width // fsdp_count
    main = experts * 16

    dispatch, combine = routing(route_ids, gate_values, cap_limit, update_ids, slot_count)
    own_columns = lax.dynamic_slice_in_dim(
        tokens.reshape(steps * rows, width), fsdp_at * share, share, axis=1
    )
    sending = jnp.dot(dispatch, own_columns, preferred_element_type=jnp.float32).astype(jnp.bfloat16)
    head = sending[:main].reshape(experts, 16, share)
    head = jnp.pad(head, ((0, 0), (0, 0), (0, 1920 - share)))
    tail = jnp.pad(sending[main:], ((0, 0), (0, 2048 - share))).reshape(experts, 8, 512)
    tail = jnp.pad(tail, ((0, 0), (0, 0), (0, 128)))
    beside = jnp.concatenate(
        [head[:, :, :640], head[:, :, 640:1280], head[:, :, 1280:], tail], axis=1
    )
    outgoing, down_raw = pack(expert_weights, beside)
    core = (fsdp_at % 2).astype(jnp.int32)
    upper = fsdp_at // 2 == 1
    second = core == 1
    outgoing, down_raw, combine, core, upper, second = lax.optimization_barrier(
        (outgoing, down_raw, combine, core, upper, second)
    )
    arrived = exchange(outgoing)
    arrived, down_raw = lax.optimization_barrier((arrived, down_raw))
    down = exchange(down_raw).reshape(share, hidden)

    passed, kept = gate_up(core.reshape(1), arrived, hidden, share)
    kept = kept + lax.ppermute(passed, "fsdp", CORE_SWAP)
    g0, g1, u0, u1 = (kept[:, i * quarter : (i + 1) * quarter] for i in range(4))
    send = jnp.concatenate([jnp.where(upper, g0, g1), jnp.where(upper, u0, u1)], axis=1)
    gate = jnp.where(upper, g1, g0)
    up = jnp.where(upper, u1, u0)
    across = lax.ppermute(send.astype(jnp.bfloat16), "fsdp", CHIP_SWAP).astype(jnp.float32)
    act = (jax.nn.silu(gate + across[:, :quarter]) * (up + across[:, quarter:])).astype(jnp.bfloat16)
    other = lax.ppermute(act, "fsdp", CHIP_SWAP)
    act = jnp.concatenate([jnp.where(upper, other, act), jnp.where(upper, act, other)], axis=1)
    other = lax.ppermute(act, "fsdp", CORE_SWAP)
    act = jnp.concatenate([jnp.where(second, other, act), jnp.where(second, act, other)], axis=1)
    out = lax.dot_general(
        act, down, (((1,), (1,)), ((), ())), preferred_element_type=jnp.float32
    ).astype(jnp.bfloat16)
    rest = out[main:].reshape(experts, 14, 256)
    rest = jnp.pad(rest, ((0, 0), (0, 2), (0, 0)))
    going = jnp.concatenate([out[:main].reshape(experts, 16, share), rest], axis=2)
    returned = exchange(going)
    mixed = jnp.dot(
        combine[:, :main],
        returned[:, :, :share].reshape(main, share),
        preferred_element_type=jnp.float32,
    ) + jnp.dot(
        combine[:, main:],
        returned[:, :14, share:].reshape(experts * 2, share),
        preferred_element_type=jnp.float32,
    )
    return mixed.astype(jnp.bfloat16).reshape(steps, rows, share)


def solution(mesh):
    return jax.shard_map(
        layer,
        mesh=mesh,
        in_specs=(
            P(None, "expert", None),
            P(None, "expert", None),
            P(None, "expert", None),
            P(),
            P(),
            P(None, ("fsdp", "expert"), None),
        ),
        out_specs=P(None, "expert", "fsdp"),
        check_vma=False,
    )
```

```python
import functools

import jax
import jax.numpy as jnp
from jax import lax
from jax.experimental import pallas as pl
from jax.experimental.pallas import tpu as pltpu
from jax.sharding import PartitionSpec as P


CORE_SWAP = ((0, 1), (1, 0), (2, 3), (3, 2))
CHIP_SWAP = ((0, 2), (2, 0), (1, 3), (3, 1))


def exchange(block):
    return lax.all_to_all(block, "expert", split_axis=0, concat_axis=0, tiled=True)


def swap_rows(block, pieces):
    size = block.shape[0] // pieces
    return jnp.concatenate(
        [lax.ppermute(block[i * size : (i + 1) * size], "fsdp", CHIP_SWAP) for i in range(pieces)]
    )


def pack_kernel(
    steps, rows, top, slot_count,
    at_ref, choices_ref, limit_ref, held_ref, tokens_ref, weights_ref,
    first_out, second_out, combine_ref, first_ref, second_ref, own, sems,
):
    experts, _, columns = weights_ref.shape
    wide = columns // 3 * 2
    share = own.shape[1]
    main = 16 * experts
    total = experts * steps * slot_count
    parts = 4
    some = [pl.ds(i * (experts // parts), experts // parts) for i in range(parts)]
    arriving, leaving = [], []
    for i in range(parts):
        inner = first_ref.at[some[i], :, pl.ds(0, wide)]
        arriving.append(
            pltpu.make_async_copy(weights_ref.at[some[i], :, pl.ds(0, wide)], inner, sems.at[0, i])
        )
        leaving.append(
            pltpu.make_async_copy(inner, first_out.at[some[i], :, pl.ds(0, wide)], sems.at[1, i])
        )
    for i in range(parts):
        arriving.append(
            pltpu.make_async_copy(
                weights_ref.at[some[i], :, pl.ds(wide, columns - wide)], second_ref.at[some[i]], sems.at[2, i]
            )
        )
        leaving.append(
            pltpu.make_async_copy(second_ref.at[some[i]], second_out.at[some[i]], sems.at[3, i])
        )
    start = pl.multiple_of(at_ref[0] * share, 128)
    fetch = pltpu.make_async_copy(tokens_ref.at[:, pl.ds(start, share)], own, sems.at[4, 0])
    fetch.start()
    for copy in arriving:
        copy.start()

    count = steps * rows * top
    ids = choices_ref[0:1, :].astype(jnp.int32)
    square = lax.broadcasted_iota(jnp.int32, (experts, experts), 1)
    diagonal = lax.broadcasted_iota(jnp.int32, (experts, experts), 0) == square
    held = jnp.sum(
        jnp.where(diagonal, held_ref[...].astype(jnp.float32), 0.0), axis=1, keepdims=True
    ).astype(jnp.int32)
    hot = held == ids
    hot32 = hot.astype(jnp.float32)
    before_of = lax.broadcasted_iota(jnp.int32, (count, count), 0)
    number = lax.broadcasted_iota(jnp.int32, (count, count), 1)
    per_step = rows * top
    earlier = (before_of < number) & (before_of >= number - (number & (per_step - 1)))
    before = jnp.dot(
        hot.astype(jnp.bfloat16), earlier.astype(jnp.bfloat16), preferred_element_type=jnp.float32
    )
    position = jnp.sum(before * hot32, axis=0, keepdims=True).astype(jnp.int32)
    named = held == square
    limit_of = jnp.sum(
        jnp.where(named, limit_ref[...].astype(jnp.float32), 0.0), axis=1, keepdims=True
    )
    limit = jnp.sum(hot32 * limit_of, axis=0, keepdims=True).astype(jnp.int32)
    holder = lax.broadcasted_iota(jnp.int32, (experts, count), 0).astype(jnp.float32)
    owner = jnp.sum(hot32 * holder, axis=0, keepdims=True).astype(jnp.int32)
    choice = lax.broadcasted_iota(jnp.int32, (1, count), 1)
    within = lax.shift_right_logical(choice, per_step.bit_length() - 1) * slot_count + position
    slot = jnp.where(within < 16, owner * 16 + within, main + owner * 2 + within - 16)
    slot = jnp.where(position < limit, slot, -1)

    row_of = lax.shift_right_logical(
        lax.broadcasted_iota(jnp.int32, (count, steps * rows), 0), top.bit_length() - 1
    )
    row_hot = (row_of == lax.broadcasted_iota(jnp.int32, (count, steps * rows), 1)).astype(jnp.bfloat16)

    def match(size, of):
        return (of(lax.broadcasted_iota(jnp.int32, (size, count), 0)) == slot).astype(jnp.bfloat16)

    top_match = match(main, lambda i: i)
    last_match = match(total - main, lambda i: i + main)
    tail_match = match(8 * experts, lambda i: main + lax.shift_right_logical(i, 2))
    choice_row = lax.shift_right_logical(
        lax.broadcasted_iota(jnp.int32, (steps * rows, count), 1), top.bit_length() - 1
    )
    here = choice_row == lax.broadcasted_iota(jnp.int32, (steps * rows, count), 0)
    weighted = jnp.where(here, choices_ref[1:2, :], 0.0).astype(jnp.bfloat16)
    contract = (((1,), (1,)), ((), ()))
    combine_ref[:, :main] = lax.dot_general(
        weighted, top_match, contract, preferred_element_type=jnp.float32
    ).astype(jnp.bfloat16)
    combine_ref[:, main:] = lax.dot_general(
        weighted, last_match, contract, preferred_element_type=jnp.float32
    ).astype(jnp.bfloat16)
    send_top = jnp.dot(top_match, row_hot, preferred_element_type=jnp.float32).astype(jnp.bfloat16)
    send_tail = jnp.dot(tail_match, row_hot, preferred_element_type=jnp.float32)
    piece_of = lax.broadcasted_iota(jnp.int32, (8 * experts, steps * rows), 0) & 3

    for here_now, onward in zip(arriving, leaving, strict=True):
        here_now.wait()
        onward.start()
    fetch.wait()
    for b in range(3):
        width = min(640, share - 640 * b)
        piece = jnp.dot(
            send_top, own[:, 640 * b : 640 * b + width], preferred_element_type=jnp.float32
        ).astype(jnp.bfloat16)
        first_ref[:, 16 * b : 16 * b + 16, wide : wide + width] = piece.reshape(experts, 16, width)
    zeros = jnp.zeros((experts, 24, 128), jnp.bfloat16)
    first_ref[:, 32:56, wide + 512 :] = zeros
    rest = jnp.zeros((8 * experts, 512), jnp.float32)
    for q in range(4):
        width = min(512, share - 512 * q)
        picked = jnp.where(piece_of == q, send_tail, 0.0).astype(jnp.bfloat16)
        piece = jnp.dot(picked, own[:, 512 * q : 512 * q + width], preferred_element_type=jnp.float32)
        if width < 512:
            piece = jnp.concatenate([piece, jnp.zeros((8 * experts, 512 - width), jnp.float32)], axis=1)
        rest = rest + piece
    first_ref[:, 48:56, wide : wide + 512] = rest.astype(jnp.bfloat16).reshape(experts, 8, 512)
    beside = pl.ds(wide, first_ref.shape[2] - wide)
    last = pltpu.make_async_copy(
        first_ref.at[:, :, beside], first_out.at[:, :, beside], sems.at[4, 1]
    )
    last.start()
    for copy in leaving:
        copy.wait()
    last.wait()


def pack(fsdp_at, tokens, route_ids, gate_values, cap_limit, update_ids, weights, slot_count, share):
    steps, rows, top = route_ids.shape
    experts, local, columns = weights.shape
    wide = columns // 3 * 2
    count = steps * rows * top
    vmem = pl.BlockSpec(memory_space=pltpu.VMEM)
    hbm = pl.BlockSpec(memory_space=pltpu.HBM)
    return pl.pallas_call(
        functools.partial(pack_kernel, steps, rows, top, slot_count),
        in_specs=[pl.BlockSpec(memory_space=pltpu.SMEM), vmem, vmem, vmem, hbm, hbm],
        out_specs=[hbm, hbm, vmem],
        out_shape=[
            jax.ShapeDtypeStruct((experts, local, wide + 640), weights.dtype),
            jax.ShapeDtypeStruct((experts, local, columns - wide), weights.dtype),
            jax.ShapeDtypeStruct((steps * rows, experts * steps * slot_count), jnp.bfloat16),
        ],
        scratch_shapes=[
            pltpu.VMEM((experts, local, wide + 640), weights.dtype),
            pltpu.VMEM((experts, local, columns - wide), weights.dtype),
            pltpu.VMEM((steps * rows, share), jnp.bfloat16),
            pltpu.SemaphoreType.DMA((5, 4)),
        ],
        compiler_params=pltpu.CompilerParams(vmem_limit_bytes=56 << 20),
        name="pack",
    )(
        fsdp_at.reshape(1),
        jnp.stack([route_ids.astype(jnp.float32), gate_values.astype(jnp.float32)]).reshape(2, count),
        cap_limit.reshape(1, experts),
        update_ids.reshape(1, experts),
        tokens.reshape(steps * rows, tokens.shape[2]),
        weights,
    )


def gate_up_kernel(core_ref, arrived_ref, passed_ref, kept_ref, weights, rows, tail, sems):
    experts, local, _ = arrived_ref.shape
    quarter = weights.shape[3]
    wide = 4 * quarter
    share = rows.shape[2]
    main = experts * 16
    core = core_ref[0]
    copies = [
        pltpu.make_async_copy(
            arrived_ref.at[:, pl.ds(16 * b, 16), pl.ds(wide, w)],
            rows.at[:, :, pl.ds(640 * b, w)],
            sems.at[b],
        )
        for b, w in enumerate((640, 640, share - 1280))
    ]
    copies.append(
        pltpu.make_async_copy(arrived_ref.at[:, pl.ds(48, 8), pl.ds(wide, 512)], tail, sems.at[3])
    )
    starts = [(1 - core) * quarter, (1 - core) * quarter + 2 * quarter]
    starts += [core * quarter, core * quarter + 2 * quarter]
    for i, start in enumerate(starts):
        copies.append(
            pltpu.make_async_copy(
                arrived_ref.at[:, :, pl.ds(pl.multiple_of(start, quarter), quarter)],
                weights.at[i],
                sems.at[4 + i],
            )
        )
    for copy in copies:
        copy.start()
    for copy in copies[:4]:
        copy.wait()
    top = rows[...].reshape(main, share)
    flat = tail[...].reshape(experts * 8, 512)
    at = lax.broadcasted_iota(jnp.int32, (2 * experts, 8 * experts), 0)
    of = lax.broadcasted_iota(jnp.int32, (2 * experts, 8 * experts), 1)
    pieces = []
    for q in range(4):
        pick = (of == at * 4 + q).astype(jnp.bfloat16)
        pieces.append(jnp.dot(pick, flat, preferred_element_type=jnp.float32).astype(jnp.bfloat16))
    last = jnp.concatenate(pieces, axis=1)[:, :share]
    for i in range(4):
        copies[4 + i].wait()
        block = weights[i].reshape(experts * local, quarter)
        out_ref = passed_ref if i < 2 else kept_ref
        columns = pl.ds((i % 2) * quarter, quarter)
        out_ref[:main, columns] = jnp.dot(top, block, preferred_element_type=jnp.float32)
        out_ref[main:, columns] = jnp.dot(last, block, preferred_element_type=jnp.float32)


def gate_up(core, arrived, hidden, share):
    experts, local, _ = arrived.shape
    slots = experts * 18
    quarter = hidden // 2
    out = jax.ShapeDtypeStruct((slots, hidden), jnp.float32)
    return pl.pallas_call(
        gate_up_kernel,
        in_specs=[
            pl.BlockSpec(memory_space=pltpu.SMEM),
            pl.BlockSpec(memory_space=pltpu.HBM),
        ],
        out_specs=[pl.BlockSpec(memory_space=pltpu.VMEM)] * 2,
        out_shape=[out, out],
        scratch_shapes=[
            pltpu.VMEM((4, experts, local, quarter), jnp.bfloat16),
            pltpu.VMEM((experts, 16, share), jnp.bfloat16),
            pltpu.VMEM((experts, 8, 512), jnp.bfloat16),
            pltpu.SemaphoreType.DMA((8,)),
        ],
        compiler_params=pltpu.CompilerParams(vmem_limit_bytes=54 << 20),
        cost_estimate=pl.CostEstimate(
            flops=2 * slots * share * 2 * hidden,
            bytes_accessed=2 * arrived.size + 8 * slots * hidden,
            transcendentals=0,
        ),
        name="gate_up",
    )(core, arrived)


def layer(tokens, route_ids, gate_values, cap_limit, update_ids, expert_weights):
    steps, rows, width = tokens.shape
    experts, _, _ = expert_weights.shape
    fsdp_count = lax.axis_size("fsdp")
    fsdp_at = lax.axis_index("fsdp").astype(jnp.int32)
    slot_count = 6
    hidden = expert_weights.shape[2] // 3
    half = hidden // 2
    quarter = half // 2
    share = width // fsdp_count
    main = experts * 16

    outgoing, down_raw, combine = pack(
        fsdp_at, tokens, route_ids, gate_values, cap_limit, update_ids, expert_weights, slot_count, share
    )
    core = (fsdp_at % 2).astype(jnp.int32)
    upper = fsdp_at // 2 == 1
    second = core == 1
    outgoing, down_raw, combine, core, upper, second = lax.optimization_barrier(
        (outgoing, down_raw, combine, core, upper, second)
    )
    arrived = exchange(outgoing)
    arrived, down_raw = lax.optimization_barrier((arrived, down_raw))
    down = exchange(down_raw).reshape(share, hidden)

    passed, kept = gate_up(core.reshape(1), arrived, hidden, share)
    kept = kept + lax.ppermute(passed, "fsdp", CORE_SWAP)
    g0, g1, u0, u1 = (kept[:, i * quarter : (i + 1) * quarter] for i in range(4))
    send = jnp.concatenate([jnp.where(upper, g0, g1), jnp.where(upper, u0, u1)], axis=1)
    gate = jnp.where(upper, g1, g0)
    up = jnp.where(upper, u1, u0)
    across = swap_rows(send.astype(jnp.bfloat16), 6).astype(jnp.float32)
    act = (jax.nn.silu(gate + across[:, :quarter]) * (up + across[:, quarter:])).astype(jnp.bfloat16)
    other = swap_rows(act, 3)
    act = jnp.concatenate([jnp.where(upper, other, act), jnp.where(upper, act, other)], axis=1)
    other = lax.ppermute(act, "fsdp", CORE_SWAP)
    act = jnp.concatenate([jnp.where(second, other, act), jnp.where(second, act, other)], axis=1)
    out = lax.dot_general(
        act, down, (((1,), (1,)), ((), ())), preferred_element_type=jnp.float32
    ).astype(jnp.bfloat16)
    rest = out[main:].reshape(experts, 14, 256)
    rest = jnp.pad(rest, ((0, 0), (0, 2), (0, 0)))
    going = jnp.concatenate([out[:main].reshape(experts, 16, share), rest], axis=2)
    returned = exchange(going)
    mixed = jnp.dot(
        combine[:, :main],
        returned[:, :, :share].reshape(main, share),
        preferred_element_type=jnp.float32,
    ) + jnp.dot(
        combine[:, main:],
        returned[:, :14, share:].reshape(experts * 2, share),
        preferred_element_type=jnp.float32,
    )
    return mixed.astype(jnp.bfloat16).reshape(steps, rows, share)


def solution(mesh):
    return jax.shard_map(
        layer,
        mesh=mesh,
        in_specs=(
            P(None, "expert", None),
            P(None, "expert", None),
            P(None, "expert", None),
            P(),
            P(),
            P(None, ("fsdp", "expert"), None),
        ),
        out_specs=P(None, "expert", "fsdp"),
        check_vma=False,
    )
```

```python
import functools

import jax
import jax.numpy as jnp
from jax import lax
from jax.experimental import pallas as pl
from jax.experimental.pallas import tpu as pltpu
from jax.sharding import PartitionSpec as P


CORE_SWAP = ((0, 1), (1, 0), (2, 3), (3, 2))
CHIP_SWAP = ((0, 2), (2, 0), (1, 3), (3, 1))


def exchange(block):
    return lax.all_to_all(block, "expert", split_axis=0, concat_axis=0, tiled=True)


def swap_rows(block, pieces):
    size = block.shape[0] // pieces
    return jnp.concatenate(
        [lax.ppermute(block[i * size : (i + 1) * size], "fsdp", CHIP_SWAP) for i in range(pieces)]
    )


def pack_kernel(
    steps, rows, top, slot_count,
    at_ref, ids_ref, gates_ref, limit_ref, held_ref, tokens_ref, weights_ref,
    first_out, second_out, combine_ref, first_ref, second_ref, own, sems,
):
    experts, _, columns = weights_ref.shape
    wide = columns // 3 * 2
    share = own.shape[1]
    main = 16 * experts
    total = experts * steps * slot_count
    parts = 4
    some = [pl.ds(i * (experts // parts), experts // parts) for i in range(parts)]
    arriving, leaving = [], []
    for i in range(parts):
        inner = first_ref.at[some[i], :, pl.ds(0, wide)]
        arriving.append(
            pltpu.make_async_copy(weights_ref.at[some[i], :, pl.ds(0, wide)], inner, sems.at[0, i])
        )
        leaving.append(
            pltpu.make_async_copy(inner, first_out.at[some[i], :, pl.ds(0, wide)], sems.at[1, i])
        )
    for i in range(parts):
        arriving.append(
            pltpu.make_async_copy(
                weights_ref.at[some[i], :, pl.ds(wide, columns - wide)], second_ref.at[some[i]], sems.at[2, i]
            )
        )
        leaving.append(
            pltpu.make_async_copy(second_ref.at[some[i]], second_out.at[some[i]], sems.at[3, i])
        )
    start = pl.multiple_of(at_ref[0] * share, 128)
    fetch = pltpu.make_async_copy(tokens_ref.at[:, pl.ds(start, share)], own, sems.at[4, 0])
    fetch.start()
    for copy in arriving:
        copy.start()

    count = steps * rows * top
    per_step = rows * top
    top_bits = top.bit_length() - 1
    step_bits = per_step.bit_length() - 1

    def in_order(values):
        named_row = lax.broadcasted_iota(jnp.int32, (rows, count), 0)
        spread_at = lax.broadcasted_iota(jnp.int32, (rows, count), 1)
        spread = (lax.shift_right_logical(spread_at, top_bits) & (rows - 1)) == named_row
        wide_values = jnp.dot(
            values.astype(jnp.bfloat16), spread.astype(jnp.bfloat16), preferred_element_type=jnp.float32
        )
        line = lax.broadcasted_iota(jnp.int32, (steps * top, count), 0)
        column = lax.broadcasted_iota(jnp.int32, (steps * top, count), 1)
        own_line = lax.shift_right_logical(column, step_bits) * top + (column & (top - 1))
        return jnp.sum(jnp.where(line == own_line, wide_values, 0.0), axis=0, keepdims=True)

    def forward(lines):
        for i in lines:
            arriving[i].wait()
            leaving[i].start()

    ids = in_order(ids_ref[...].astype(jnp.float32)).astype(jnp.int32)
    gates = in_order(gates_ref[...])
    square = lax.broadcasted_iota(jnp.int32, (experts, experts), 1)
    diagonal = lax.broadcasted_iota(jnp.int32, (experts, experts), 0) == square
    held = jnp.sum(
        jnp.where(diagonal, held_ref[...].astype(jnp.float32), 0.0), axis=1, keepdims=True
    ).astype(jnp.int32)
    hot = held == ids
    hot32 = hot.astype(jnp.float32)
    before_of = lax.broadcasted_iota(jnp.int32, (count, count), 0)
    number = lax.broadcasted_iota(jnp.int32, (count, count), 1)
    earlier = (before_of < number) & (before_of >= number - (number & (per_step - 1)))
    before = jnp.dot(
        hot.astype(jnp.bfloat16), earlier.astype(jnp.bfloat16), preferred_element_type=jnp.float32
    )
    position = jnp.sum(before * hot32, axis=0, keepdims=True).astype(jnp.int32)
    forward(range(0, 3))
    named = held == square
    limit_of = jnp.sum(
        jnp.where(named, limit_ref[...].astype(jnp.float32), 0.0), axis=1, keepdims=True
    )
    limit = jnp.sum(hot32 * limit_of, axis=0, keepdims=True).astype(jnp.int32)
    holder = lax.broadcasted_iota(jnp.int32, (experts, count), 0).astype(jnp.float32)
    owner = jnp.sum(hot32 * holder, axis=0, keepdims=True).astype(jnp.int32)
    choice = lax.broadcasted_iota(jnp.int32, (1, count), 1)
    within = lax.shift_right_logical(choice, step_bits) * slot_count + position
    slot = jnp.where(within < 16, owner * 16 + within, main + owner * 2 + within - 16)
    slot = jnp.where(position < limit, slot, -1)

    forward(range(3, 5))
    row_of = lax.shift_right_logical(
        lax.broadcasted_iota(jnp.int32, (count, steps * rows), 0), top.bit_length() - 1
    )
    row_hot = (row_of == lax.broadcasted_iota(jnp.int32, (count, steps * rows), 1)).astype(jnp.bfloat16)

    def match(size, of):
        return (of(lax.broadcasted_iota(jnp.int32, (size, count), 0)) == slot).astype(jnp.bfloat16)

    top_match = match(main, lambda i: i)
    last_match = match(total - main, lambda i: i + main)
    tail_match = match(8 * experts, lambda i: main + lax.shift_right_logical(i, 2))
    choice_row = lax.shift_right_logical(
        lax.broadcasted_iota(jnp.int32, (steps * rows, count), 1), top.bit_length() - 1
    )
    here = choice_row == lax.broadcasted_iota(jnp.int32, (steps * rows, count), 0)
    weighted = jnp.where(here, gates, 0.0).astype(jnp.bfloat16)
    contract = (((1,), (1,)), ((), ()))
    combine_ref[:, :main] = lax.dot_general(
        weighted, top_match, contract, preferred_element_type=jnp.float32
    ).astype(jnp.bfloat16)
    combine_ref[:, main:] = lax.dot_general(
        weighted, last_match, contract, preferred_element_type=jnp.float32
    ).astype(jnp.bfloat16)
    forward(range(5, 2 * parts))
    send_top = jnp.dot(top_match, row_hot, preferred_element_type=jnp.float32).astype(jnp.bfloat16)
    send_tail = jnp.dot(tail_match, row_hot, preferred_element_type=jnp.float32)
    piece_of = lax.broadcasted_iota(jnp.int32, (8 * experts, steps * rows), 0) & 3

    fetch.wait()
    for b in range(3):
        width = min(640, share - 640 * b)
        piece = jnp.dot(
            send_top, own[:, 640 * b : 640 * b + width], preferred_element_type=jnp.float32
        ).astype(jnp.bfloat16)
        first_ref[:, 16 * b : 16 * b + 16, wide : wide + width] = piece.reshape(experts, 16, width)
    zeros = jnp.zeros((experts, 24, 128), jnp.bfloat16)
    first_ref[:, 32:56, wide + 512 :] = zeros
    rest = jnp.zeros((8 * experts, 512), jnp.float32)
    for q in range(4):
        width = min(512, share - 512 * q)
        picked = jnp.where(piece_of == q, send_tail, 0.0).astype(jnp.bfloat16)
        piece = jnp.dot(picked, own[:, 512 * q : 512 * q + width], preferred_element_type=jnp.float32)
        if width < 512:
            piece = jnp.concatenate([piece, jnp.zeros((8 * experts, 512 - width), jnp.float32)], axis=1)
        rest = rest + piece
    first_ref[:, 48:56, wide : wide + 512] = rest.astype(jnp.bfloat16).reshape(experts, 8, 512)
    beside = pl.ds(wide, first_ref.shape[2] - wide)
    last = pltpu.make_async_copy(
        first_ref.at[:, :, beside], first_out.at[:, :, beside], sems.at[4, 1]
    )
    last.start()
    for copy in leaving:
        copy.wait()
    last.wait()


def pack(fsdp_at, tokens, route_ids, gate_values, cap_limit, update_ids, weights, slot_count, share):
    steps, rows, top = route_ids.shape
    experts, local, columns = weights.shape
    wide = columns // 3 * 2
    vmem = pl.BlockSpec(memory_space=pltpu.VMEM)
    hbm = pl.BlockSpec(memory_space=pltpu.HBM)
    return pl.pallas_call(
        functools.partial(pack_kernel, steps, rows, top, slot_count),
        in_specs=[pl.BlockSpec(memory_space=pltpu.SMEM), vmem, vmem, vmem, vmem, hbm, hbm],
        out_specs=[hbm, hbm, vmem],
        out_shape=[
            jax.ShapeDtypeStruct((experts, local, wide + 640), weights.dtype),
            jax.ShapeDtypeStruct((experts, local, columns - wide), weights.dtype),
            jax.ShapeDtypeStruct((steps * rows, experts * steps * slot_count), jnp.bfloat16),
        ],
        scratch_shapes=[
            pltpu.VMEM((experts, local, wide + 640), weights.dtype),
            pltpu.VMEM((experts, local, columns - wide), weights.dtype),
            pltpu.VMEM((steps * rows, share), jnp.bfloat16),
            pltpu.SemaphoreType.DMA((5, 4)),
        ],
        compiler_params=pltpu.CompilerParams(vmem_limit_bytes=56 << 20),
        name="pack",
    )(
        fsdp_at.reshape(1),
        route_ids.transpose(0, 2, 1).reshape(steps * top, rows),
        gate_values.transpose(0, 2, 1).reshape(steps * top, rows),
        cap_limit.reshape(1, experts),
        update_ids.reshape(1, experts),
        tokens.reshape(steps * rows, tokens.shape[2]),
        weights,
    )


def gate_up_kernel(core_ref, arrived_ref, passed_ref, kept_ref, weights, rows, tail, sems):
    experts, local, _ = arrived_ref.shape
    quarter = weights.shape[3]
    wide = 4 * quarter
    share = rows.shape[2]
    main = experts * 16
    core = core_ref[0]
    copies = [
        pltpu.make_async_copy(
            arrived_ref.at[:, pl.ds(16 * b, 16), pl.ds(wide, w)],
            rows.at[:, :, pl.ds(640 * b, w)],
            sems.at[b],
        )
        for b, w in enumerate((640, 640, share - 1280))
    ]
    copies.append(
        pltpu.make_async_copy(arrived_ref.at[:, pl.ds(48, 8), pl.ds(wide, 512)], tail, sems.at[3])
    )
    starts = [(1 - core) * quarter, (1 - core) * quarter + 2 * quarter]
    starts += [core * quarter, core * quarter + 2 * quarter]
    for i, start in enumerate(starts):
        copies.append(
            pltpu.make_async_copy(
                arrived_ref.at[:, :, pl.ds(pl.multiple_of(start, quarter), quarter)],
                weights.at[i],
                sems.at[4 + i],
            )
        )
    for copy in copies:
        copy.start()
    for copy in copies[:4]:
        copy.wait()
    top = rows[...].reshape(main, share)
    flat = tail[...].reshape(experts * 8, 512)
    at = lax.broadcasted_iota(jnp.int32, (2 * experts, 8 * experts), 0)
    of = lax.broadcasted_iota(jnp.int32, (2 * experts, 8 * experts), 1)
    pieces = []
    for q in range(4):
        pick = (of == at * 4 + q).astype(jnp.bfloat16)
        pieces.append(jnp.dot(pick, flat, preferred_element_type=jnp.float32).astype(jnp.bfloat16))
    last = jnp.concatenate(pieces, axis=1)[:, :share]
    for i in range(4):
        copies[4 + i].wait()
        block = weights[i].reshape(experts * local, quarter)
        out_ref = passed_ref if i < 2 else kept_ref
        columns = pl.ds((i % 2) * quarter, quarter)
        out_ref[:main, columns] = jnp.dot(top, block, preferred_element_type=jnp.float32)
        out_ref[main:, columns] = jnp.dot(last, block, preferred_element_type=jnp.float32)


def gate_up(core, arrived, hidden, share):
    experts, local, _ = arrived.shape
    slots = experts * 18
    quarter = hidden // 2
    out = jax.ShapeDtypeStruct((slots, hidden), jnp.float32)
    return pl.pallas_call(
        gate_up_kernel,
        in_specs=[
            pl.BlockSpec(memory_space=pltpu.SMEM),
            pl.BlockSpec(memory_space=pltpu.HBM),
        ],
        out_specs=[pl.BlockSpec(memory_space=pltpu.VMEM)] * 2,
        out_shape=[out, out],
        scratch_shapes=[
            pltpu.VMEM((4, experts, local, quarter), jnp.bfloat16),
            pltpu.VMEM((experts, 16, share), jnp.bfloat16),
            pltpu.VMEM((experts, 8, 512), jnp.bfloat16),
            pltpu.SemaphoreType.DMA((8,)),
        ],
        compiler_params=pltpu.CompilerParams(vmem_limit_bytes=54 << 20),
        cost_estimate=pl.CostEstimate(
            flops=2 * slots * share * 2 * hidden,
            bytes_accessed=2 * arrived.size + 8 * slots * hidden,
            transcendentals=0,
        ),
        name="gate_up",
    )(core, arrived)


def layer(tokens, route_ids, gate_values, cap_limit, update_ids, expert_weights):
    steps, rows, width = tokens.shape
    experts, _, _ = expert_weights.shape
    fsdp_count = lax.axis_size("fsdp")
    fsdp_at = lax.axis_index("fsdp").astype(jnp.int32)
    slot_count = 6
    hidden = expert_weights.shape[2] // 3
    half = hidden // 2
    quarter = half // 2
    share = width // fsdp_count
    main = experts * 16

    outgoing, down_raw, combine = pack(
        fsdp_at, tokens, route_ids, gate_values, cap_limit, update_ids, expert_weights, slot_count, share
    )
    core = (fsdp_at % 2).astype(jnp.int32)
    upper = fsdp_at // 2 == 1
    second = core == 1
    outgoing, down_raw, combine, core, upper, second = lax.optimization_barrier(
        (outgoing, down_raw, combine, core, upper, second)
    )
    arrived = exchange(outgoing)
    arrived, down_raw = lax.optimization_barrier((arrived, down_raw))
    down = exchange(down_raw).reshape(share, hidden)

    passed, kept = gate_up(core.reshape(1), arrived, hidden, share)
    kept = kept + lax.ppermute(passed, "fsdp", CORE_SWAP)
    g0, g1, u0, u1 = (kept[:, i * quarter : (i + 1) * quarter] for i in range(4))
    send = jnp.concatenate([jnp.where(upper, g0, g1), jnp.where(upper, u0, u1)], axis=1)
    gate = jnp.where(upper, g1, g0)
    up = jnp.where(upper, u1, u0)
    across = swap_rows(send.astype(jnp.bfloat16), 6).astype(jnp.float32)
    act = (jax.nn.silu(gate + across[:, :quarter]) * (up + across[:, quarter:])).astype(jnp.bfloat16)
    other = swap_rows(act, 3)
    act = jnp.concatenate([jnp.where(upper, other, act), jnp.where(upper, act, other)], axis=1)
    other = lax.ppermute(act, "fsdp", CORE_SWAP)
    act = jnp.concatenate([jnp.where(second, other, act), jnp.where(second, act, other)], axis=1)
    out = lax.dot_general(
        act, down, (((1,), (1,)), ((), ())), preferred_element_type=jnp.float32
    ).astype(jnp.bfloat16)
    rest = out[main:].reshape(experts, 14, 256)
    rest = jnp.pad(rest, ((0, 0), (0, 2), (0, 0)))
    going = jnp.concatenate([out[:main].reshape(experts, 16, share), rest], axis=2)
    returned = exchange(going)
    mixed = jnp.dot(
        combine[:, :main],
        returned[:, :, :share].reshape(main, share),
        preferred_element_type=jnp.float32,
    ) + jnp.dot(
        combine[:, main:],
        returned[:, :14, share:].reshape(experts * 2, share),
        preferred_element_type=jnp.float32,
    )
    return mixed.astype(jnp.bfloat16).reshape(steps, rows, share)


def solution(mesh):
    return jax.shard_map(
        layer,
        mesh=mesh,
        in_specs=(
            P(None, "expert", None),
            P(None, "expert", None),
            P(None, "expert", None),
            P(),
            P(),
            P(None, ("fsdp", "expert"), None),
        ),
        out_specs=P(None, "expert", "fsdp"),
        check_vma=False,
    )
```

```python
import functools

import jax
import jax.numpy as jnp
from jax import lax
from jax.experimental import pallas as pl
from jax.experimental.pallas import tpu as pltpu
from jax.sharding import PartitionSpec as P


CORE_SWAP = ((0, 1), (1, 0), (2, 3), (3, 2))
CHIP_SWAP = ((0, 2), (2, 0), (1, 3), (3, 1))


def exchange(block):
    return lax.all_to_all(block, "expert", split_axis=0, concat_axis=0, tiled=True)


def swap_rows(block, pieces):
    size = block.shape[0] // pieces
    return jnp.concatenate(
        [lax.ppermute(block[i * size : (i + 1) * size], "fsdp", CHIP_SWAP) for i in range(pieces)]
    )


def pack_kernel(
    steps, rows, top, slot_count,
    at_ref, ids_ref, gates_ref, limit_ref, held_ref, tokens_ref, weights_ref,
    first_out, second_out, combine_ref, first_ref, second_ref, own, sems,
):
    experts, _, columns = weights_ref.shape
    wide = columns // 3 * 2
    share = own.shape[1]
    main = 16 * experts
    total = experts * steps * slot_count
    parts = 4
    some = [pl.ds(i * (experts // parts), experts // parts) for i in range(parts)]
    arriving, leaving = [], []
    for i in range(parts):
        inner = first_ref.at[some[i], :, pl.ds(0, wide)]
        arriving.append(
            pltpu.make_async_copy(weights_ref.at[some[i], :, pl.ds(0, wide)], inner, sems.at[0, i])
        )
        leaving.append(
            pltpu.make_async_copy(inner, first_out.at[some[i], :, pl.ds(0, wide)], sems.at[1, i])
        )
    for i in range(parts):
        arriving.append(
            pltpu.make_async_copy(
                weights_ref.at[some[i], :, pl.ds(wide, columns - wide)], second_ref.at[some[i]], sems.at[2, i]
            )
        )
        leaving.append(
            pltpu.make_async_copy(second_ref.at[some[i]], second_out.at[some[i]], sems.at[3, i])
        )
    start = pl.multiple_of(at_ref[0] * share, 128)
    fetch = pltpu.make_async_copy(tokens_ref.at[:, pl.ds(start, share)], own, sems.at[4, 0])
    fetch.start()
    for copy in arriving:
        copy.start()

    count = steps * rows * top
    per_step = rows * top
    top_bits = top.bit_length() - 1
    step_bits = per_step.bit_length() - 1

    def in_order(values):
        named_row = lax.broadcasted_iota(jnp.int32, (rows, count), 0)
        spread_at = lax.broadcasted_iota(jnp.int32, (rows, count), 1)
        spread = (lax.shift_right_logical(spread_at, top_bits) & (rows - 1)) == named_row
        wide_values = jnp.dot(
            values.astype(jnp.bfloat16), spread.astype(jnp.bfloat16), preferred_element_type=jnp.float32
        )
        line = lax.broadcasted_iota(jnp.int32, (steps * top, count), 0)
        column = lax.broadcasted_iota(jnp.int32, (steps * top, count), 1)
        own_line = lax.shift_right_logical(column, step_bits) * top + (column & (top - 1))
        return jnp.sum(jnp.where(line == own_line, wide_values, 0.0), axis=0, keepdims=True)

    def forward(lines):
        for i in lines:
            arriving[i].wait()
            leaving[i].start()

    ids = in_order(ids_ref[...].astype(jnp.float32)).astype(jnp.int32)
    gates = in_order(gates_ref[...])
    square = lax.broadcasted_iota(jnp.int32, (experts, experts), 1)
    diagonal = lax.broadcasted_iota(jnp.int32, (experts, experts), 0) == square
    held = jnp.sum(
        jnp.where(diagonal, held_ref[...].astype(jnp.float32), 0.0), axis=1, keepdims=True
    ).astype(jnp.int32)
    hot = held == ids
    hot32 = hot.astype(jnp.float32)
    before_of = lax.broadcasted_iota(jnp.int32, (count, count), 0)
    number = lax.broadcasted_iota(jnp.int32, (count, count), 1)
    earlier = (before_of < number) & (before_of >= number - (number & (per_step - 1)))
    before = jnp.dot(
        hot.astype(jnp.bfloat16), earlier.astype(jnp.bfloat16), preferred_element_type=jnp.float32
    )
    position = jnp.sum(before * hot32, axis=0, keepdims=True).astype(jnp.int32)
    forward(range(0, 3))
    named = held == square
    limit_of = jnp.sum(
        jnp.where(named, limit_ref[...].astype(jnp.float32), 0.0), axis=1, keepdims=True
    )
    limit = jnp.sum(hot32 * limit_of, axis=0, keepdims=True).astype(jnp.int32)
    holder = lax.broadcasted_iota(jnp.int32, (experts, count), 0).astype(jnp.float32)
    owner = jnp.sum(hot32 * holder, axis=0, keepdims=True).astype(jnp.int32)
    choice = lax.broadcasted_iota(jnp.int32, (1, count), 1)
    within = lax.shift_right_logical(choice, step_bits) * slot_count + position
    slot = jnp.where(within < 16, owner * 16 + within, main + owner * 2 + within - 16)
    slot = jnp.where(position < limit, slot, -1)

    forward(range(3, 5))
    row_of = lax.shift_right_logical(
        lax.broadcasted_iota(jnp.int32, (count, steps * rows), 0), top.bit_length() - 1
    )
    row_hot = (row_of == lax.broadcasted_iota(jnp.int32, (count, steps * rows), 1)).astype(jnp.bfloat16)

    def match(size, of):
        return (of(lax.broadcasted_iota(jnp.int32, (size, count), 0)) == slot).astype(jnp.bfloat16)

    top_match = match(main, lambda i: i)
    last_match = match(total - main, lambda i: i + main)
    tail_match = match(8 * experts, lambda i: main + lax.shift_right_logical(i, 2))
    choice_row = lax.shift_right_logical(
        lax.broadcasted_iota(jnp.int32, (steps * rows, count), 1), top.bit_length() - 1
    )
    here = choice_row == lax.broadcasted_iota(jnp.int32, (steps * rows, count), 0)
    weighted = jnp.where(here, gates, 0.0).astype(jnp.bfloat16)
    contract = (((1,), (1,)), ((), ()))
    combine_ref[:, :main] = lax.dot_general(
        weighted, top_match, contract, preferred_element_type=jnp.float32
    ).astype(jnp.bfloat16)
    combine_ref[:, main:] = lax.dot_general(
        weighted, last_match, contract, preferred_element_type=jnp.float32
    ).astype(jnp.bfloat16)
    forward(range(5, 2 * parts))
    send_top = jnp.dot(top_match, row_hot, preferred_element_type=jnp.float32).astype(jnp.bfloat16)
    send_tail = jnp.dot(tail_match, row_hot, preferred_element_type=jnp.float32)
    piece_of = lax.broadcasted_iota(jnp.int32, (8 * experts, steps * rows), 0) & 3

    fetch.wait()
    for b in range(3):
        width = min(640, share - 640 * b)
        piece = jnp.dot(
            send_top, own[:, 640 * b : 640 * b + width], preferred_element_type=jnp.float32
        ).astype(jnp.bfloat16)
        first_ref[:, 16 * b : 16 * b + 16, wide : wide + width] = piece.reshape(experts, 16, width)
    zeros = jnp.zeros((experts, 24, 128), jnp.bfloat16)
    first_ref[:, 32:56, wide + 512 :] = zeros
    rest = jnp.zeros((8 * experts, 512), jnp.float32)
    for q in range(4):
        width = min(512, share - 512 * q)
        picked = jnp.where(piece_of == q, send_tail, 0.0).astype(jnp.bfloat16)
        piece = jnp.dot(picked, own[:, 512 * q : 512 * q + width], preferred_element_type=jnp.float32)
        if width < 512:
            piece = jnp.concatenate([piece, jnp.zeros((8 * experts, 512 - width), jnp.float32)], axis=1)
        rest = rest + piece
    first_ref[:, 48:56, wide : wide + 512] = rest.astype(jnp.bfloat16).reshape(experts, 8, 512)
    beside = pl.ds(wide, first_ref.shape[2] - wide)
    last = pltpu.make_async_copy(
        first_ref.at[:, :, beside], first_out.at[:, :, beside], sems.at[4, 1]
    )
    last.start()
    for copy in leaving:
        copy.wait()
    last.wait()


def pack(fsdp_at, tokens, route_ids, gate_values, cap_limit, update_ids, weights, slot_count, share):
    steps, rows, top = route_ids.shape
    experts, local, columns = weights.shape
    wide = columns // 3 * 2
    vmem = pl.BlockSpec(memory_space=pltpu.VMEM)
    hbm = pl.BlockSpec(memory_space=pltpu.HBM)
    return pl.pallas_call(
        functools.partial(pack_kernel, steps, rows, top, slot_count),
        in_specs=[pl.BlockSpec(memory_space=pltpu.SMEM), vmem, vmem, vmem, vmem, hbm, hbm],
        out_specs=[hbm, hbm, vmem],
        out_shape=[
            jax.ShapeDtypeStruct((experts, local, wide + 640), weights.dtype),
            jax.ShapeDtypeStruct((experts, local, columns - wide), weights.dtype),
            jax.ShapeDtypeStruct((steps * rows, experts * steps * slot_count), jnp.bfloat16),
        ],
        scratch_shapes=[
            pltpu.VMEM((experts, local, wide + 640), weights.dtype),
            pltpu.VMEM((experts, local, columns - wide), weights.dtype),
            pltpu.VMEM((steps * rows, share), jnp.bfloat16),
            pltpu.SemaphoreType.DMA((5, 4)),
        ],
        compiler_params=pltpu.CompilerParams(vmem_limit_bytes=56 << 20),
        name="pack",
    )(
        fsdp_at.reshape(1),
        route_ids.transpose(0, 2, 1).reshape(steps * top, rows),
        gate_values.transpose(0, 2, 1).reshape(steps * top, rows),
        cap_limit.reshape(1, experts),
        update_ids.reshape(1, experts),
        tokens.reshape(steps * rows, tokens.shape[2]),
        weights,
    )


def gate_up_kernel(core_ref, arrived_ref, passed_ref, kept_ref, weights, rows, tail, sems):
    experts, local, _ = arrived_ref.shape
    quarter = weights.shape[3]
    wide = 4 * quarter
    share = rows.shape[2]
    main = experts * 16
    core = core_ref[0]
    copies = [
        pltpu.make_async_copy(
            arrived_ref.at[:, pl.ds(16 * b, 16), pl.ds(wide, w)],
            rows.at[:, :, pl.ds(640 * b, w)],
            sems.at[b],
        )
        for b, w in enumerate((640, 640, share - 1280))
    ]
    copies.append(
        pltpu.make_async_copy(arrived_ref.at[:, pl.ds(48, 8), pl.ds(wide, 512)], tail, sems.at[3])
    )
    starts = [(1 - core) * quarter, (1 - core) * quarter + 2 * quarter]
    starts += [core * quarter, core * quarter + 2 * quarter]
    for i, start in enumerate(starts):
        copies.append(
            pltpu.make_async_copy(
                arrived_ref.at[:, :, pl.ds(pl.multiple_of(start, quarter), quarter)],
                weights.at[i],
                sems.at[4 + i],
            )
        )
    for copy in copies:
        copy.start()
    for copy in copies[:4]:
        copy.wait()
    top = rows[...].reshape(main, share)
    flat = tail[...].reshape(experts * 8, 512)
    at = lax.broadcasted_iota(jnp.int32, (2 * experts, 8 * experts), 0)
    of = lax.broadcasted_iota(jnp.int32, (2 * experts, 8 * experts), 1)
    pieces = []
    for q in range(4):
        pick = (of == at * 4 + q).astype(jnp.bfloat16)
        pieces.append(jnp.dot(pick, flat, preferred_element_type=jnp.float32).astype(jnp.bfloat16))
    last = jnp.concatenate(pieces, axis=1)[:, :share]
    for i in range(4):
        copies[4 + i].wait()
        block = weights[i].reshape(experts * local, quarter)
        out_ref = passed_ref if i < 2 else kept_ref
        columns = pl.ds((i % 2) * quarter, quarter)
        out_ref[:main, columns] = jnp.dot(top, block, preferred_element_type=jnp.float32)
        out_ref[main:, columns] = jnp.dot(last, block, preferred_element_type=jnp.float32)


def gate_up(core, arrived, hidden, share):
    experts, local, _ = arrived.shape
    slots = experts * 18
    quarter = hidden // 2
    out = jax.ShapeDtypeStruct((slots, hidden), jnp.float32)
    return pl.pallas_call(
        gate_up_kernel,
        in_specs=[
            pl.BlockSpec(memory_space=pltpu.SMEM),
            pl.BlockSpec(memory_space=pltpu.HBM),
        ],
        out_specs=[pl.BlockSpec(memory_space=pltpu.VMEM)] * 2,
        out_shape=[out, out],
        scratch_shapes=[
            pltpu.VMEM((4, experts, local, quarter), jnp.bfloat16),
            pltpu.VMEM((experts, 16, share), jnp.bfloat16),
            pltpu.VMEM((experts, 8, 512), jnp.bfloat16),
            pltpu.SemaphoreType.DMA((8,)),
        ],
        compiler_params=pltpu.CompilerParams(vmem_limit_bytes=54 << 20),
        cost_estimate=pl.CostEstimate(
            flops=2 * slots * share * 2 * hidden,
            bytes_accessed=2 * arrived.size + 8 * slots * hidden,
            transcendentals=0,
        ),
        name="gate_up",
    )(core, arrived)


def own_down_kernel(core_ref, act_ref, down_ref, out_ref, weights, sems):
    parts, size, half = weights.shape
    columns = pl.ds(pl.multiple_of(core_ref[0] * half, half), half)
    copies = [
        pltpu.make_async_copy(down_ref.at[pl.ds(i * size, size), columns], weights.at[i], sems.at[i])
        for i in range(parts)
    ]
    for copy in copies:
        copy.start()
    for i, copy in enumerate(copies):
        copy.wait()
        out_ref[:, i * size : (i + 1) * size] = lax.dot_general(
            act_ref[...], weights[i], (((1,), (1,)), ((), ())), preferred_element_type=jnp.float32
        )


def own_down(core, act, down):
    slots, half = act.shape
    share = down.shape[0]
    parts = 2
    return pl.pallas_call(
        own_down_kernel,
        in_specs=[
            pl.BlockSpec(memory_space=pltpu.SMEM),
            pl.BlockSpec(memory_space=pltpu.VMEM),
            pl.BlockSpec(memory_space=pltpu.HBM),
        ],
        out_specs=pl.BlockSpec(memory_space=pltpu.VMEM),
        out_shape=jax.ShapeDtypeStruct((slots, share), jnp.float32),
        scratch_shapes=[
            pltpu.VMEM((parts, share // parts, half), down.dtype),
            pltpu.SemaphoreType.DMA((parts,)),
        ],
        compiler_params=pltpu.CompilerParams(vmem_limit_bytes=24 << 20),
        cost_estimate=pl.CostEstimate(
            flops=2 * slots * share * half,
            bytes_accessed=2 * half * share + 4 * slots * share,
            transcendentals=0,
        ),
        name="own_down",
    )(core, act, down)


def layer(tokens, route_ids, gate_values, cap_limit, update_ids, expert_weights):
    steps, rows, width = tokens.shape
    experts, _, _ = expert_weights.shape
    fsdp_count = lax.axis_size("fsdp")
    fsdp_at = lax.axis_index("fsdp").astype(jnp.int32)
    slot_count = 6
    hidden = expert_weights.shape[2] // 3
    half = hidden // 2
    quarter = half // 2
    share = width // fsdp_count
    main = experts * 16

    outgoing, down_raw, combine = pack(
        fsdp_at, tokens, route_ids, gate_values, cap_limit, update_ids, expert_weights, slot_count, share
    )
    core = (fsdp_at % 2).astype(jnp.int32)
    upper = fsdp_at // 2 == 1
    outgoing, down_raw, combine, core, upper = lax.optimization_barrier(
        (outgoing, down_raw, combine, core, upper)
    )
    arrived = exchange(outgoing)
    arrived, down_raw = lax.optimization_barrier((arrived, down_raw))
    down = exchange(down_raw).reshape(share, hidden)

    passed, kept = gate_up(core.reshape(1), arrived, hidden, share)
    kept = kept + lax.ppermute(passed, "fsdp", CORE_SWAP)
    g0, g1, u0, u1 = (kept[:, i * quarter : (i + 1) * quarter] for i in range(4))
    send = jnp.concatenate([jnp.where(upper, g0, g1), jnp.where(upper, u0, u1)], axis=1)
    gate = jnp.where(upper, g1, g0)
    up = jnp.where(upper, u1, u0)
    across = swap_rows(send.astype(jnp.bfloat16), 6).astype(jnp.float32)
    act = (jax.nn.silu(gate + across[:, :quarter]) * (up + across[:, quarter:])).astype(jnp.bfloat16)
    other = swap_rows(act, 3)
    act = jnp.concatenate([jnp.where(upper, other, act), jnp.where(upper, act, other)], axis=1)
    other = lax.ppermute(act, "fsdp", CORE_SWAP)
    own_part = own_down(core.reshape(1), act, down)
    other_down = lax.dynamic_slice_in_dim(down, (1 - core) * half, half, axis=1)
    out = own_part + lax.dot_general(
        other, other_down, (((1,), (1,)), ((), ())), preferred_element_type=jnp.float32
    )
    out = out.astype(jnp.bfloat16)
    rest = out[main:].reshape(experts, 14, 256)
    rest = jnp.pad(rest, ((0, 0), (0, 2), (0, 0)))
    going = jnp.concatenate([out[:main].reshape(experts, 16, share), rest], axis=2)
    returned = exchange(going)
    mixed = jnp.dot(
        combine[:, :main],
        returned[:, :, :share].reshape(main, share),
        preferred_element_type=jnp.float32,
    ) + jnp.dot(
        combine[:, main:],
        returned[:, :14, share:].reshape(experts * 2, share),
        preferred_element_type=jnp.float32,
    )
    return mixed.astype(jnp.bfloat16).reshape(steps, rows, share)


def solution(mesh):
    return jax.shard_map(
        layer,
        mesh=mesh,
        in_specs=(
            P(None, "expert", None),
            P(None, "expert", None),
            P(None, "expert", None),
            P(),
            P(),
            P(None, ("fsdp", "expert"), None),
        ),
        out_specs=P(None, "expert", "fsdp"),
        check_vma=False,
    )
```
